32 devices in a mesh: seq: 16 (over z, y, core), tp: 2 (over x).
Axes of the slice: x: 2, y: 2, z: 4, core: 2. Of those that a mesh axis runs over, the one named last changes fastest.
Arguments:
- tokens: bfloat16 [8192, 2048], P('seq'), may hold values from -6 to 6
- doc_lengths: int32 [1, 32], replicated, may hold values from 1 to 768, 8192 in all within a row
- gain_one: bfloat16 [2048], P('seq'), may hold values from 0.099609375 to 1.8984375
- w_qkv: bfloat16 [2048, 3, 2048], P('seq', None, 'tp'), may hold values from -0.125 to 0.125
- w_out: bfloat16 [2048, 2048], P('tp', 'seq'), may hold values from -0.375 to 0.375
- gain_two: bfloat16 [2048], P('seq'), may hold values from 0.099609375 to 1.8984375
- w_gate_up: bfloat16 [2048, 2, 5504], P('seq', None, 'tp'), may hold values from -0.125 to 0.125
- w_down: bfloat16 [5504, 2048], P('tp', 'seq'), may hold values from -0.078125 to 0.078125
- cotangent: bfloat16 [8192, 2048], P('seq'), may hold values from -6 to 6
Outputs:
- result: bfloat16 [8192, 2048], P('seq')
- grad_tokens: float32 [8192, 2048], P('seq')
- grad_gain_one: float32 [2048], P('seq')
- grad_w_qkv: float32 [2048, 3, 2048], P('seq', None, 'tp')
- grad_w_out: float32 [2048, 2048], P('tp', 'seq')
- grad_gain_two: float32 [2048], P('seq')
- grad_w_gate_up: float32 [2048, 2, 5504], P('seq', None, 'tp')
- grad_w_down: float32 [5504, 2048], P('tp', 'seq')
The draws below stay inside these ranges and needn't reach their ends.
Inputs may be any that keep to these rules, and one draw needn't show every extreme that they name: `doc_lengths`: each row lists the lengths of its 32 documents in order; they fill the row's 8192 tokens, and the longest document of every row has exactly 768 tokens.
All inputs are finite; a program needn't handle non-finite values.
Results may differ from the reference program's by a relative error of at most 0.014.
Values may be sent and summed in bfloat16 or wider, within the bound.
No kernel may reach another device: no remote copies, remote signals or barrier semaphores. Data moves between devices by JAX's collectives and lax.ppermute only.
A program may use at most 256 MiB of HBM per device.

```python
import math
import jax
import jax.numpy as jnp
import numpy as np
from jax import lax

D = 2048
HEADS = 16
HEAD_DIM = 128
FF = 5504
WINDOW = 64
DOC_MOST = 768
TOKENS = 8192
ROW = 8192
ROWS = 1
NDOC = 32


def spiked(result, key, source, target, blocks, factor):
    def block_of(position):
        return (jnp.arange(result.shape[position]) // (result.shape[position] // blocks)).reshape((-1,) + (1,) * (result.ndim - 1 - position))

    one_side = jax.random.permutation(key, blocks)[block_of(target)]
    other_side = (block_of(target) + blocks // 2) % blocks
    return jnp.where((block_of(source) == one_side) | (block_of(source) == other_side), factor * result, result)


def steps_of(stream_key, extent, pieces, least, high):
    def one(dim, blocks):
        heights = jax.random.uniform(jax.random.fold_in(jax.random.fold_in(stream_key, 6), dim), (blocks,), jnp.float32, least / len(pieces), high / len(pieces))
        return jnp.repeat(jnp.exp(heights), extent[dim] // blocks).reshape((-1,) + (1,) * (len(extent) - dim - 1))

    loudness = one(*pieces[0])
    for cut in pieces[1:]:
        loudness = loudness * one(*cut)
    return loudness


def profile(number_of, total, most, slope):
    weights = [(1 << 20) // math.isqrt(grade ** slope) + 1 for grade in range(2, number_of + 1)]
    rest, counts = total - most - (number_of - 1), [1] * (number_of - 1)
    while rest > 0:
        free = [i for i in range(number_of - 1) if counts[i] < most]
        whole, budget = sum([weights[i] for i in free]), rest
        for i in free:
            more = min(most - counts[i], max(1, budget * weights[i] // whole), rest)
            counts[i] = counts[i] + more
            rest = rest - more
    return np.array([most] + counts)


def uneven(own_key, amount, total, bound, lean):
    if amount == 2:
        one = jax.random.randint(own_key, (), max(1, total - bound), min(bound, total - 1) + 1)
        return jnp.stack([one, total - one])
    tallies = jnp.asarray(profile(amount, total, bound, lean), jnp.int32)
    twos = (amount - 1) // 2
    donor, sink = tallies[1:1 + 2 * twos:2], tallies[2:2 + 2 * twos:2]
    margin = jnp.minimum(donor - 1, bound - sink)
    shifted = jax.random.randint(jax.random.fold_in(own_key, 1), (twos,), 0, 1 << 20) % (margin + 1)
    tallies = tallies.at[1:1 + 2 * twos:2].set(donor - shifted).at[2:2 + 2 * twos:2].set(sink + shifted)
    return tallies[jax.random.permutation(jax.random.fold_in(own_key, 2), amount)]


def noise(stream_key, extent, width, limit, cuts=(), kind=jnp.bfloat16):
    entries = jax.random.normal(stream_key, extent, jnp.float32) * width
    if len(cuts) > 0:
        entries = steps_of(stream_key, extent, cuts, -0.22, 0.18) * entries
    return jnp.clip(entries, min=-limit, max=limit).astype(kind)


def bell_draw_with(key, shape, deviation, limit, pieces, heavy, kind=jnp.bfloat16):
    drawn = deviation * jax.random.normal(key, shape, jnp.float32)
    if pieces:
        drawn = drawn * steps_of(key, shape, pieces, -0.22, 0.18)
    return jnp.clip(spiked(drawn, jax.random.fold_in(key, 3), *heavy), -limit, limit).astype(kind)


def setup_inputs(seed: int = 0) -> dict:
    streams_of = jax.random.split(jax.random.key(seed), 10)
    return {
        "tokens": bell_draw_with(streams_of[0], (TOKENS, D), 1.0, 6.0, ((0, 16),), (0, 1, 16, 2.0)),
        "doc_lengths": jax.vmap(lambda own: uneven(own, NDOC, ROW, DOC_MOST, 2))(jax.random.split(streams_of[1], ROWS)).reshape((ROWS, NDOC)).astype(jnp.int32),
        "gain_one": jnp.clip(1.0 + 0.18 * jax.random.normal(streams_of[2], (D,), jnp.float32), 0.099609375, 1.8984375).astype(jnp.bfloat16),
        "w_qkv": noise(streams_of[3], (D, 3, D), D ** -0.5, 0.125, ((0, 16), (2, 2))),
        "w_out": noise(streams_of[4], (D, D), (D // 8) ** -0.5, 0.375, ((0, 2), (1, 16))),
        "gain_two": jnp.clip(1.0 + 0.18 * jax.random.normal(streams_of[5], (D,), jnp.float32), 0.099609375, 1.8984375).astype(jnp.bfloat16),
        "w_gate_up": noise(streams_of[6], (D, 2, FF), D ** -0.5, 0.125, ((0, 16), (2, 2))),
        "w_down": noise(streams_of[7], (FF, D), FF ** -0.5, 0.078125, ((0, 2), (1, 16))),
        "cotangent": bell_draw_with(streams_of[8], (TOKENS, D), 1.0, 6.0, ((0, 16),), (0, 1, 16, 2.0)),
    }


@jax.custom_vjp
def low(v):
    return lax.optimization_barrier(v.astype(jnp.bfloat16)).astype(jnp.float32)

@jax.custom_vjp
def low_back(v):
    return v

def low_keep(v):
    return (low(v), None)

def low_pass(kept, grad):
    return (grad,)

def back_keep(v):
    return (v, None)

def back_low(kept, grad):
    return (low(grad),)
low.defvjp(low_keep, low_pass)
low_back.defvjp(back_keep, back_low)
EPSILON = 1e-05
NEGATIVE = -1e+30
precise_mode = lax.Precision.HIGHEST

def rms_scale(values_in, gain_vec):
    return values_in * lax.rsqrt(lax.optimization_barrier(jnp.mean(values_in * values_in, axis=-1, keepdims=True)) + EPSILON) * gain_vec

def doc_starts(lengths, positions):
    doc_ends = jnp.cumsum(lengths)
    return lax.optimization_barrier(jnp.sum(jnp.where(doc_ends[None, :] <= positions[:, None], lengths[None, :], 0), axis=1)).astype(jnp.int32)

def block_mask(query_pos, key_pos, block_starts):
    return (key_pos[None, :] >= block_starts[:, None]) & (key_pos[None, :] <= query_pos[:, None]) & (query_pos[:, None] - key_pos[None, :] < WINDOW)

def attend_row(queries, key_rows, values, starts):
    block_rows = min(512, ROW)
    score_scale = HEAD_DIM ** (-0.5)
    zero_pad = jnp.zeros((WINDOW, HEADS, HEAD_DIM), jnp.float32)
    keys_ext = jnp.concatenate([zero_pad, key_rows], axis=0)
    values_ext = jnp.concatenate([zero_pad, values], axis=0)

    def attend_block(block_start):
        query_block = lax.dynamic_slice_in_dim(queries, block_start, block_rows, 0)
        key_block = lax.dynamic_slice_in_dim(keys_ext, block_start, block_rows + WINDOW, 0)
        value_block = lax.dynamic_slice_in_dim(values_ext, block_start, block_rows + WINDOW, 0)
        query_pos = block_start + jnp.arange(block_rows, dtype=jnp.int32)
        key_pos = block_start - WINDOW + jnp.arange(block_rows + WINDOW, dtype=jnp.int32)
        block_starts = lax.dynamic_slice_in_dim(starts, block_start, block_rows, 0)
        scores = low_back(jnp.einsum('qhd,khd->hqk', query_block, key_block, precision=precise_mode) * score_scale)
        scores = jnp.where(block_mask(query_pos, key_pos, block_starts)[None], scores, NEGATIVE)
        row_max = lax.optimization_barrier(jnp.max(scores, axis=-1, keepdims=True))
        exponent = jnp.exp(scores - row_max)
        probabilities = low(exponent / lax.optimization_barrier(jnp.sum(exponent, axis=-1, keepdims=True)))
        return jnp.einsum('hqk,khd->qhd', probabilities, value_block, precision=precise_mode)
    block_firsts = jnp.arange(ROW // block_rows, dtype=jnp.int32) * block_rows
    block_outs = lax.map(jax.checkpoint(attend_block), block_firsts)
    return block_outs.reshape(ROW, HEADS * HEAD_DIM)

def layer_row(row_tokens, gain_one, w_qkv, w_out, gain_two, w_gate_up, w_down, starts):
    normed = low(rms_scale(row_tokens, gain_one))
    proj_qkv = low(low_back(jnp.einsum('td,dcf->tcf', normed, w_qkv, precision=precise_mode)))
    head_shape = (ROW, HEADS, HEAD_DIM)
    attn_mixed = attend_row(proj_qkv[:, 0].reshape(head_shape), proj_qkv[:, 1].reshape(head_shape), proj_qkv[:, 2].reshape(head_shape), starts)
    attn_mixed = low(low_back(attn_mixed))
    attn_out = low_back(jnp.dot(attn_mixed, w_out, precision=precise_mode))
    middle = row_tokens + attn_out
    normed_two = low(rms_scale(middle, gain_two))
    gate_up = low_back(jnp.einsum('td,dcf->tcf', normed_two, w_gate_up, precision=precise_mode))
    gate_part = gate_up[:, 0]
    hidden = low(gate_part / (1.0 + jnp.exp(-gate_part)) * gate_up[:, 1])
    return middle + low_back(jnp.dot(hidden, w_down, precision=precise_mode))

def reference(tokens, doc_lengths, gain_one, w_qkv, w_out, gain_two, w_gate_up, w_down, cotangent):
    weights = tuple((weight.astype(jnp.float32) for weight in (gain_one, w_qkv, w_out, gain_two, w_gate_up, w_down)))
    token_rows = tokens.astype(jnp.float32).reshape(ROWS, ROW, D)
    cot_rows = cotangent.astype(jnp.float32).reshape(ROWS, ROW, D)
    positions = jnp.arange(ROW, dtype=jnp.int32)

    def row_step(totals, scan_item):
        row_tokens, cot_row, lengths = scan_item
        starts = doc_starts(lengths, positions)

        def forward(row_in, *weight_list):
            return layer_row(row_in, *weight_list, starts)
        row_out, pullback = jax.vjp(forward, row_tokens, *weights)
        grad_list = pullback(cot_row)
        new_totals = tuple((total_grad + one_grad for total_grad, one_grad in zip(totals, grad_list[1:])))
        return (new_totals, (row_out, grad_list[0]))
    zero_grads = tuple((jnp.zeros(weight.shape, jnp.float32) for weight in weights))
    totals, (row_outs, grad_rows) = lax.scan(row_step, zero_grads, (token_rows, cot_rows, doc_lengths))
    return (row_outs.reshape(TOKENS, D).astype(jnp.bfloat16), grad_rows.reshape(TOKENS, D), totals[0], totals[1], totals[2], totals[3], totals[4], totals[5])
```

```python
import jax
import jax.numpy as jnp
from jax import lax
from jax.sharding import PartitionSpec as P

HEAD_DIM = 128
WINDOW = 64


EPSILON = 1e-05
NEGATIVE = -1e30


def shifted(block, axis, distance):
    devices = range(lax.axis_size(axis))
    route = [(i - distance, i) for i in devices if i - distance in devices]
    return lax.ppermute(block, axis, route)


def scattered(terms, dimension):
    low = terms.astype(jnp.bfloat16)
    return lax.psum_scatter(low, "seq", scatter_dimension=dimension, tiled=True).astype(jnp.float32)


def rms_scale(values_in, gain_vec):
    return (
        values_in
        * lax.rsqrt(jnp.mean(values_in * values_in, axis=-1, keepdims=True) + EPSILON)
        * gain_vec
    )


def gated(gate_part, up_part):
    return gate_part / (1.0 + jnp.exp(-gate_part)) * up_part


def doc_starts(lengths, positions):
    doc_ends = jnp.cumsum(lengths)
    return jnp.sum(jnp.where(doc_ends[None, :] <= positions[:, None], lengths[None, :], 0), axis=1)


def block_mask(query_pos, key_pos, block_starts):
    return (
        (key_pos[None, :] >= block_starts[:, None])
        & (key_pos[None, :] <= query_pos[:, None])
        & (query_pos[:, None] - key_pos[None, :] < WINDOW)
    )


def local(tokens, doc_lengths, gain_one, w_qkv, w_out, gain_two, w_gate_up, w_down, cotangent):
    token_count = tokens.shape[0]
    local_width = w_qkv.shape[2]
    local_heads = local_width // HEAD_DIM
    score_scale = HEAD_DIM ** (-0.5)
    block_rows = min(512, token_count)
    row_length = token_count * lax.axis_size("seq") // doc_lengths.shape[0]
    first_token = lax.axis_index("seq") * token_count
    lengths = doc_lengths[0]
    positions = first_token % row_length + jnp.arange(token_count, dtype=jnp.int32)
    starts = doc_starts(lengths, positions)
    f32 = jnp.float32
    bf16 = jnp.bfloat16
    qkv_full, gain_one_full, out_full = (
        lax.all_gather(w_qkv, "seq", axis=0, tiled=True),
        lax.all_gather(gain_one, "seq", axis=0, tiled=True),
        lax.all_gather(w_out, "seq", axis=1, tiled=True),
    )
    token_rows = tokens.astype(f32)
    gain_a = gain_one_full.astype(f32)
    normed = rms_scale(token_rows, gain_a).astype(bf16)
    proj_qkv = jnp.einsum("td,dcf->tcf", normed, qkv_full, preferred_element_type=f32).astype(bf16)
    queries = proj_qkv[:, 0]
    key_rows = proj_qkv[:, 1]
    values = proj_qkv[:, 2]
    key_rim = jnp.stack([key_rows[token_count - WINDOW :], values[token_count - WINDOW :]])
    before = shifted(key_rim, "seq", 1)
    keys_ext = jnp.concatenate([before[0], key_rows], axis=0)
    values_ext = jnp.concatenate([before[1], values], axis=0)

    def scores_for():
        query_block = queries.reshape(block_rows, local_heads, HEAD_DIM)
        key_block = keys_ext.reshape(block_rows + WINDOW, local_heads, HEAD_DIM)
        value_block = values_ext.reshape(block_rows + WINDOW, local_heads, HEAD_DIM)
        key_pos = positions[0] - WINDOW + jnp.arange(block_rows + WINDOW, dtype=jnp.int32)
        scores = (
            jnp.einsum("qhd,khd->hqk", query_block, key_block, preferred_element_type=f32)
            * score_scale
        )
        scores = jnp.where(block_mask(positions, key_pos, starts)[None], scores, NEGATIVE)
        return (query_block, key_block, value_block, scores)

    def attend(block_start):
        query_block, key_block, value_block, scores = scores_for()
        row_max = jnp.max(scores, axis=-1, keepdims=True)
        exponent = jnp.exp(scores - row_max)
        row_total = jnp.sum(exponent, axis=-1, keepdims=True)
        probabilities = (exponent / row_total).astype(bf16)
        block_out = jnp.einsum(
            "hqk,khd->qhd", probabilities, value_block, preferred_element_type=f32
        )
        return (block_out.reshape(block_rows, local_width), (row_max + jnp.log(row_total))[..., 0])

    block_firsts = jnp.arange(token_count // block_rows, dtype=jnp.int32) * block_rows
    mixed_blocks, log_totals = lax.map(attend, block_firsts)
    attn_mixed = mixed_blocks.reshape(token_count, local_width).astype(bf16)
    attn_out = lax.psum(
        jnp.dot(attn_mixed, out_full, preferred_element_type=f32).astype(bf16), "tp"
    ).astype(f32)
    middle = token_rows + attn_out
    gate_up_full, gain_two_full, down_full = (
        lax.all_gather(w_gate_up, "seq", axis=0, tiled=True),
        lax.all_gather(gain_two, "seq", axis=0, tiled=True),
        lax.all_gather(w_down, "seq", axis=1, tiled=True),
    )
    gain_b = gain_two_full.astype(f32)
    normed_two = rms_scale(middle, gain_b).astype(bf16)
    gate_up = jnp.einsum("td,dcf->tcf", normed_two, gate_up_full, preferred_element_type=f32)
    gate_part = gate_up[:, 0]
    up_part = gate_up[:, 1]
    hidden = gated(gate_part, up_part).astype(bf16)
    branch = lax.psum(
        jnp.dot(hidden, down_full, preferred_element_type=f32).astype(jnp.bfloat16), "tp"
    ).astype(jnp.float32)
    result = (middle + branch).astype(bf16)
    gate_up_back, gain_two_back, down_back = (
        lax.all_gather(w_gate_up, "seq", axis=0, tiled=True),
        lax.all_gather(gain_two, "seq", axis=0, tiled=True),
        lax.all_gather(w_down, "seq", axis=1, tiled=True),
    )
    qkv_back, gain_one_back, out_back = (
        lax.all_gather(w_qkv, "seq", axis=0, tiled=True),
        lax.all_gather(gain_one, "seq", axis=0, tiled=True),
        lax.all_gather(w_out, "seq", axis=1, tiled=True),
    )
    gain_b = gain_two_back.astype(f32)
    gain_a = gain_one_back.astype(f32)
    grad_w_down = jnp.einsum("tf,td->fd", hidden, cotangent, preferred_element_type=f32)
    grad_hidden = jnp.einsum("td,fd->tf", cotangent, down_back, preferred_element_type=f32)
    unused_value, gate_pull = jax.vjp(gated, gate_part, up_part)
    grad_gate, grad_up = gate_pull(grad_hidden)
    grad_gate_up = jnp.stack([grad_gate, grad_up], axis=1).astype(bf16)
    grad_w_gate_up = jnp.einsum("td,tcf->dcf", normed_two, grad_gate_up, preferred_element_type=f32)
    grad_normed_two = lax.psum(
        jnp.einsum("tcf,dcf->td", grad_gate_up, gate_up_back, preferred_element_type=f32).astype(
            bf16
        ),
        "tp",
    ).astype(f32)
    unused_norm, norm_pull = jax.vjp(rms_scale, middle, gain_b)
    grad_mid_norm, grad_gain_two = norm_pull(grad_normed_two)
    grad_middle = cotangent.astype(f32) + grad_mid_norm
    mlp_terms = (grad_w_gate_up, grad_gain_two, grad_w_down)
    mlp_grads = (
        scattered(mlp_terms[0], 0),
        lax.psum_scatter(mlp_terms[1], "seq", scatter_dimension=0, tiled=True),
        scattered(mlp_terms[2], 1),
    )
    grad_attn = grad_middle.astype(bf16)
    grad_w_out = jnp.einsum("tf,td->fd", attn_mixed, grad_attn, preferred_element_type=f32)
    grad_mixed = jnp.einsum("td,fd->tf", grad_attn, out_back, preferred_element_type=f32).astype(
        bf16
    )

    def attend_back(carried, scan_item):
        grad_keys_ext, grad_values_ext = carried
        block_start, block_totals = scan_item
        query_block, key_block, value_block, scores = scores_for()
        probabilities = jnp.exp(scores - block_totals[..., None])
        grad_block = grad_mixed.reshape(block_rows, local_heads, HEAD_DIM)
        grad_probs = jnp.einsum("qhd,khd->hqk", grad_block, value_block, preferred_element_type=f32)
        grad_value_block = jnp.einsum(
            "hqk,qhd->khd", probabilities.astype(bf16), grad_block, preferred_element_type=f32
        )
        row_inner = jnp.sum(probabilities * grad_probs, axis=-1, keepdims=True)
        grad_scores = (probabilities * (grad_probs - row_inner)).astype(bf16)
        grad_query_block = (
            jnp.einsum("hqk,khd->qhd", grad_scores, key_block, preferred_element_type=f32)
            * score_scale
        )
        grad_key_block = (
            jnp.einsum("hqk,qhd->khd", grad_scores, query_block, preferred_element_type=f32)
            * score_scale
        )
        span = block_rows + WINDOW
        old_keys = grad_keys_ext
        old_values = grad_values_ext
        grad_keys_ext = old_keys + grad_key_block.reshape(span, local_width)
        grad_values_ext = old_values + grad_value_block.reshape(span, local_width)
        return ((grad_keys_ext, grad_values_ext), grad_query_block.reshape(block_rows, local_width))

    zero_ext = jnp.zeros((token_count + WINDOW, local_width), f32)
    (grad_keys_ext, grad_values_ext), grad_query_blocks = lax.scan(
        attend_back, (zero_ext, zero_ext), (block_firsts, log_totals)
    )
    grad_queries = grad_query_blocks.reshape(token_count, local_width)
    edge_grads = jnp.stack([grad_keys_ext[:WINDOW], grad_values_ext[:WINDOW]])
    arrived = shifted(edge_grads.astype(jnp.bfloat16), "seq", -1).astype(edge_grads.dtype)
    grad_keys = grad_keys_ext[WINDOW:].at[token_count - WINDOW :].add(arrived[0])
    grad_values = grad_values_ext[WINDOW:].at[token_count - WINDOW :].add(arrived[1])
    grad_proj = jnp.stack([grad_queries, grad_keys, grad_values], axis=1).astype(bf16)
    grad_w_qkv = jnp.einsum("td,tcf->dcf", normed, grad_proj, preferred_element_type=f32)
    grad_normed = lax.psum(
        jnp.einsum("tcf,dcf->td", grad_proj, qkv_back, preferred_element_type=f32).astype(bf16),
        "tp",
    ).astype(f32)
    unused_first, first_pull = jax.vjp(rms_scale, token_rows, gain_a)
    grad_rows_norm, grad_gain_one = first_pull(grad_normed)
    grad_tokens = grad_middle + grad_rows_norm
    attn_grads = (
        scattered(grad_w_qkv, 0),
        lax.psum_scatter(grad_gain_one, "seq", scatter_dimension=0, tiled=True),
        scattered(grad_w_out, 1),
    )
    return (
        result,
        grad_tokens,
        attn_grads[1],
        attn_grads[0],
        attn_grads[2],
        mlp_grads[1],
        mlp_grads[0],
        mlp_grads[2],
    )


def solution(mesh):
    return jax.shard_map(
        local,
        mesh=mesh,
        in_specs=(
            P("seq", None),
            P(),
            P("seq"),
            P("seq", None, "tp"),
            P("tp", "seq"),
            P("seq"),
            P("seq", None, "tp"),
            P("tp", "seq"),
            P("seq", None),
        ),
        out_specs=(
            P("seq", None),
            P("seq", None),
            P("seq"),
            P("seq", None, "tp"),
            P("tp", "seq"),
            P("seq"),
            P("seq", None, "tp"),
            P("tp", "seq"),
        ),
        check_vma=False,
    )
```

```python
import jax
import jax.numpy as jnp
from jax import lax
from jax.sharding import PartitionSpec as P

HEAD_DIM = 128
WINDOW = 64


EPSILON = 1e-05
NEGATIVE = -1e30


def shifted(block, axis, distance):
    devices = range(lax.axis_size(axis))
    route = [(i - distance, i) for i in devices if i - distance in devices]
    return lax.ppermute(block, axis, route)


def chip_at(place, chips):
    place = place % chips
    return jnp.where(place < chips // 2, 2 * place, 2 * chips - 1 - 2 * place)


def ring_routes(chips):
    cycle = list(range(0, chips, 2)) + list(range(1, chips, 2))[::-1]
    ahead = []
    for place in range(chips):
        for core in range(2):
            ahead.append((2 * cycle[place] + core, 2 * cycle[(place + 1) % chips] + core))
    return ahead, [(target, source) for source, target in ahead]


def ring_scatter(terms, chips, place):
    routes = ring_routes(chips)
    steps = (1, -1)

    def part(direction, offset):
        chip = chip_at(place - steps[direction] * offset, chips)
        start = (chip, direction, 0, 0)
        return lax.dynamic_slice(terms, start, (1, 1) + terms.shape[2:])[0, 0]

    sums = [part(direction, 1) for direction in range(2)]
    for hop in range(2, chips + 1):
        for direction in range(2):
            arrived = lax.ppermute(sums[direction], "seq", routes[direction])
            total = arrived.astype(jnp.float32) + part(direction, hop).astype(jnp.float32)
            sums[direction] = total if hop == chips else total.astype(jnp.bfloat16)
    return jnp.concatenate(sums, axis=0)


def partner(block):
    size = lax.axis_size("seq")
    return lax.ppermute(block, "seq", [(i, i ^ 1) for i in range(size)])


def pair_rows(block):
    return jnp.concatenate([block, partner(block)], axis=0)


def pair_columns(block, chips, core):
    split = block.reshape(block.shape[0], chips, 2, -1)
    kept = lax.dynamic_index_in_dim(split, core, 2, keepdims=False)
    given = lax.dynamic_index_in_dim(split, 1 - core, 2, keepdims=False)
    both = jnp.concatenate([kept, partner(given)], axis=0)
    return both.reshape(both.shape[0], -1)


def pair_terms(left, right, chips):
    terms = jnp.einsum("td,tf->df", left, right, preferred_element_type=jnp.float32)
    rows = left.shape[1] // chips
    return terms.astype(jnp.bfloat16).reshape(chips, 2, rows // 2, right.shape[1])


def tp_sum(partial):
    sent = lax.optimization_barrier(partial.astype(jnp.bfloat16))
    other = lax.ppermute(sent, "tp", [(0, 1), (1, 0)])
    return sent.astype(jnp.float32) + other.astype(jnp.float32)


def gather_small(block):
    size = lax.axis_size("seq")
    index = lax.axis_index("seq")
    bit = 1
    while bit < size:
        other = lax.ppermute(block, "seq", [(i, i ^ bit) for i in range(size)])
        low_side = jnp.concatenate([block, other], axis=-1)
        high_side = jnp.concatenate([other, block], axis=-1)
        block = jnp.where(index & bit != 0, high_side, low_side)
        bit *= 2
    return block


def scatter_small(block):
    size = lax.axis_size("seq")
    index = lax.axis_index("seq")
    bit = size // 2
    while bit > 0:
        low_side, high_side = jnp.split(block, 2)
        upper = index & bit != 0
        given = jnp.where(upper, low_side, high_side)
        other = lax.ppermute(given, "seq", [(i, i ^ bit) for i in range(size)])
        block = jnp.where(upper, high_side, low_side) + other
        bit //= 2
    return block


def windows(rows, count, span):
    return jnp.stack([rows[i * span : (i + 1) * span + WINDOW] for i in range(count)])


def rms_scale(values_in, gain_vec):
    return (
        values_in
        * lax.rsqrt(jnp.mean(values_in * values_in, axis=-1, keepdims=True) + EPSILON)
        * gain_vec
    )


def gated(gate_part, up_part):
    return gate_part / (1.0 + jnp.exp(-gate_part)) * up_part


def doc_starts(lengths, positions):
    doc_ends = jnp.cumsum(lengths)
    return jnp.sum(jnp.where(doc_ends[None, :] <= positions[:, None], lengths[None, :], 0), axis=1)


def local(tokens, doc_lengths, gain_one, w_qkv, w_out, gain_two, w_gate_up, w_down, cotangent):
    token_count = tokens.shape[0]
    width = tokens.shape[1]
    local_width = w_qkv.shape[2]
    heads = local_width // HEAD_DIM
    score_scale = HEAD_DIM ** (-0.5)
    span = 128
    count = token_count // span
    device = lax.axis_index("seq")
    chips = lax.axis_size("seq") // 2
    core = device % 2
    chip = device // 2
    place = jnp.where(chip % 2 == 0, chip // 2, chips - (chip + 1) // 2)
    row_length = token_count * lax.axis_size("seq") // doc_lengths.shape[0]
    lengths = doc_lengths[0]
    positions = (device * token_count) % row_length + jnp.arange(token_count, dtype=jnp.int32)
    starts = doc_starts(lengths, positions)
    f32 = jnp.float32
    bf16 = jnp.bfloat16

    gains = gather_small(jnp.stack([gain_one, gain_two])).astype(f32)
    gain_a = gains[0]
    gain_b = gains[1]
    qkv_full = lax.all_gather(w_qkv, "seq", axis=0, tiled=True)
    out_full = lax.all_gather(w_out.T, "seq", axis=0, tiled=True)
    down_full = lax.all_gather(w_down.T, "seq", axis=0, tiled=True)
    gate_up_full = lax.all_gather(w_gate_up, "seq", axis=0, tiled=True)

    token_rows = tokens.astype(f32)
    normed = rms_scale(token_rows, gain_a).astype(bf16)
    proj_qkv = jnp.einsum("td,dcf->tcf", normed, qkv_full, preferred_element_type=f32).astype(bf16)
    queries = proj_qkv[:, 0]
    key_rows = proj_qkv[:, 1]
    values = proj_qkv[:, 2]
    key_rim = jnp.stack([key_rows[token_count - WINDOW :], values[token_count - WINDOW :]])
    before = shifted(key_rim, "seq", 1)
    query_blocks = queries.reshape(count, span, heads, HEAD_DIM)
    key_blocks = windows(jnp.concatenate([before[0], key_rows]), count, span)
    key_blocks = key_blocks.reshape(count, span + WINDOW, heads, HEAD_DIM)
    value_blocks = windows(jnp.concatenate([before[1], values]), count, span)
    value_blocks = value_blocks.reshape(count, span + WINDOW, heads, HEAD_DIM)
    query_pos = positions.reshape(count, span, 1)
    key_pos = query_pos[:, :1] - WINDOW + jnp.arange(span + WINDOW, dtype=jnp.int32)
    mask = (
        (key_pos >= starts.reshape(count, span, 1))
        & (key_pos <= query_pos)
        & (query_pos - key_pos < WINDOW)
    )
    scores = (
        jnp.einsum("bqhd,bkhd->bhqk", query_blocks, key_blocks, preferred_element_type=f32)
        * score_scale
    )
    scores = jnp.where(mask[:, None], scores, NEGATIVE)
    exponent = jnp.exp(scores - jnp.max(scores, axis=-1, keepdims=True))
    probabilities = exponent / jnp.sum(exponent, axis=-1, keepdims=True)
    probs_low = probabilities.astype(bf16)
    attn_mixed = (
        jnp.einsum("bhqk,bkhd->bqhd", probs_low, value_blocks, preferred_element_type=f32)
        .reshape(token_count, local_width)
        .astype(bf16)
    )
    attn_out = tp_sum(jnp.einsum("tf,df->td", attn_mixed, out_full, preferred_element_type=f32))
    middle = token_rows + attn_out
    normed_two = rms_scale(middle, gain_b).astype(bf16)
    gate_up = jnp.einsum("td,dcf->tcf", normed_two, gate_up_full, preferred_element_type=f32)
    gate_part = gate_up[:, 0]
    up_part = gate_up[:, 1]
    hidden = gated(gate_part, up_part).astype(bf16)
    cot_pair = pair_columns(cotangent, chips, core)
    down_terms = pair_terms(cot_pair, pair_rows(hidden), chips)
    grad_w_down = ring_scatter(down_terms, chips, place).T

    grad_hidden = jnp.einsum("td,df->tf", cotangent, down_full, preferred_element_type=f32)
    unused_value, gate_pull = jax.vjp(gated, gate_part, up_part)
    grad_gate, grad_up = gate_pull(grad_hidden)
    grad_gate = grad_gate.astype(bf16)
    grad_up = grad_up.astype(bf16)
    normed_pair = pair_columns(normed_two, chips, core)
    gate_terms = pair_terms(normed_pair, pair_rows(grad_gate), chips)
    up_terms = pair_terms(normed_pair, pair_rows(grad_up), chips)
    grad_w_gate = ring_scatter(gate_terms, chips, place)
    grad_w_up = ring_scatter(up_terms, chips, place)
    grad_w_gate_up = jnp.stack([grad_w_gate, grad_w_up], axis=1)
    grad_gate_up = jnp.stack([grad_gate, grad_up], axis=1)
    grad_normed_two = tp_sum(
        jnp.einsum("tcf,dcf->td", grad_gate_up, gate_up_full, preferred_element_type=f32)
    )
    branch = tp_sum(jnp.einsum("tf,df->td", hidden, down_full, preferred_element_type=f32))
    result = (middle + branch).astype(bf16)

    unused_norm, norm_pull = jax.vjp(rms_scale, middle, gain_b)
    grad_mid_norm, grad_gain_two = norm_pull(grad_normed_two)
    grad_middle = cotangent.astype(f32) + grad_mid_norm
    grad_gain_two = scatter_small(grad_gain_two)
    grad_attn = grad_middle.astype(bf16)
    grad_mixed = jnp.einsum("td,df->tf", grad_attn, out_full, preferred_element_type=f32).astype(
        bf16
    )
    out_terms = pair_terms(pair_columns(grad_attn, chips, core), pair_rows(attn_mixed), chips)
    grad_w_out = ring_scatter(out_terms, chips, place).T

    grad_blocks = grad_mixed.reshape(count, span, heads, HEAD_DIM)
    grad_probs = jnp.einsum("bqhd,bkhd->bhqk", grad_blocks, value_blocks, preferred_element_type=f32)
    grad_value_win = jnp.einsum(
        "bhqk,bqhd->bkhd", probs_low, grad_blocks, preferred_element_type=f32
    )
    row_inner = jnp.sum(probabilities * grad_probs, axis=-1, keepdims=True)
    grad_scores = (probabilities * (grad_probs - row_inner)).astype(bf16)
    grad_queries = (
        jnp.einsum("bhqk,bkhd->bqhd", grad_scores, key_blocks, preferred_element_type=f32)
        * score_scale
    )
    grad_key_win = (
        jnp.einsum("bhqk,bqhd->bkhd", grad_scores, query_blocks, preferred_element_type=f32)
        * score_scale
    )
    grad_key_win = grad_key_win.reshape(count, span + WINDOW, local_width)
    grad_value_win = grad_value_win.reshape(count, span + WINDOW, local_width)
    edge_grads = jnp.stack([grad_key_win[0, :WINDOW], grad_value_win[0, :WINDOW]])
    arrived = shifted(edge_grads.astype(bf16), "seq", -1).astype(f32)

    def joined(grad_win, edge):
        tails = jnp.concatenate([grad_win[1:, :WINDOW], edge[None]])
        own = grad_win[:, WINDOW:]
        own = jnp.concatenate([own[:, : span - WINDOW], own[:, span - WINDOW :] + tails], axis=1)
        return own.reshape(token_count, local_width)

    grad_keys = joined(grad_key_win, arrived[0])
    grad_values = joined(grad_value_win, arrived[1])
    grad_queries = grad_queries.reshape(token_count, local_width)
    grad_proj = jnp.concatenate([grad_queries, grad_keys, grad_values], axis=1).astype(bf16)
    qkv_terms = pair_terms(pair_columns(normed, chips, core), pair_rows(grad_proj), chips)
    grad_w_qkv = ring_scatter(qkv_terms, chips, place).reshape(-1, 3, local_width)
    grad_normed = tp_sum(
        jnp.einsum(
            "tf,df->td",
            grad_proj,
            qkv_full.reshape(width, 3 * local_width),
            preferred_element_type=f32,
        )
    )
    unused_first, first_pull = jax.vjp(rms_scale, token_rows, gain_a)
    grad_rows_norm, grad_gain_one = first_pull(grad_normed)
    grad_tokens = grad_middle + grad_rows_norm
    grad_gain_one = scatter_small(grad_gain_one)
    return (
        result,
        grad_tokens,
        grad_gain_one,
        grad_w_qkv,
        grad_w_out,
        grad_gain_two,
        grad_w_gate_up,
        grad_w_down,
    )


def solution(mesh):
    return jax.shard_map(
        local,
        mesh=mesh,
        in_specs=(
            P("seq", None),
            P(),
            P("seq"),
            P("seq", None, "tp"),
            P("tp", "seq"),
            P("seq"),
            P("seq", None, "tp"),
            P("tp", "seq"),
            P("seq", None),
        ),
        out_specs=(
            P("seq", None),
            P("seq", None),
            P("seq"),
            P("seq", None, "tp"),
            P("tp", "seq"),
            P("seq"),
            P("seq", None, "tp"),
            P("tp", "seq"),
        ),
        check_vma=False,
    )
```

```python
import jax
import jax.numpy as jnp
from jax import lax
from jax.experimental import pallas as pl
from jax.experimental.pallas import tpu as pltpu
from jax.sharding import PartitionSpec as P

HEAD_DIM = 128
WINDOW = 64


EPSILON = 1e-05
NEGATIVE = -1e30


def shifted(block, axis, distance):
    devices = range(lax.axis_size(axis))
    route = [(i - distance, i) for i in devices if i - distance in devices]
    return lax.ppermute(block, axis, route)


def chip_at(place, chips):
    place = place % chips
    return jnp.where(place < chips // 2, 2 * place, 2 * chips - 1 - 2 * place)


def ring_routes(chips):
    cycle = list(range(0, chips, 2)) + list(range(1, chips, 2))[::-1]
    ahead = []
    for place in range(chips):
        for core in range(2):
            ahead.append((2 * cycle[place] + core, 2 * cycle[(place + 1) % chips] + core))
    return ahead, [(target, source) for source, target in ahead]


def ring_scatter(terms, chips, place):
    routes = ring_routes(chips)
    steps = (1, -1)

    def part(direction, offset):
        chip = chip_at(place - steps[direction] * offset, chips)
        start = (chip, direction, 0, 0, 0)
        return lax.dynamic_slice(terms, start, (1, 1) + terms.shape[2:])[0, 0]

    sums = [part(direction, 1) for direction in range(2)]
    for hop in range(2, chips + 1):
        for direction in range(2):
            arrived = lax.ppermute(sums[direction], "seq", routes[direction])
            total = arrived.astype(jnp.float32) + part(direction, hop).astype(jnp.float32)
            sums[direction] = total if hop == chips else total.astype(jnp.bfloat16)
    return jnp.concatenate(sums, axis=1)


def partner(block):
    size = lax.axis_size("seq")
    return lax.ppermute(block, "seq", [(i, i ^ 1) for i in range(size)])


def select_kernel(core_ref, own_ref, other_ref, kept_ref, given_ref):
    kept_ref[...] = own_ref[...]
    given_ref[...] = other_ref[...]


def pair_columns(block, chips, core):
    tokens, width = block.shape
    rows = width // (2 * chips)
    half = jax.ShapeDtypeStruct((tokens, width // 2), block.dtype)
    if rows % 128 == 0:
        kept, given = pl.pallas_call(
            select_kernel,
            grid_spec=pltpu.PrefetchScalarGridSpec(
                num_scalar_prefetch=1,
                grid=(chips,),
                in_specs=[
                    pl.BlockSpec((tokens, rows), lambda q, c: (0, 2 * q + c[0])),
                    pl.BlockSpec((tokens, rows), lambda q, c: (0, 2 * q + 1 - c[0])),
                ],
                out_specs=[pl.BlockSpec((tokens, rows), lambda q, c: (0, q))] * 2,
            ),
            out_shape=[half, half],
            name="select_columns",
        )(core.reshape(1), block, block)
    else:
        split = block.reshape(tokens, chips, 2, rows)
        kept = lax.dynamic_index_in_dim(split, core, 2, keepdims=False).reshape(half.shape)
        given = lax.dynamic_index_in_dim(split, 1 - core, 2, keepdims=False).reshape(half.shape)
    return kept, partner(given)


def pair_kernel(left_ref, left_two_ref, right_ref, right_two_ref, terms_ref):
    def product(left, right):
        return lax.dot_general(
            left, right, (((0,), (0,)), ((), ())), preferred_element_type=jnp.float32
        )

    total = product(left_ref[...], right_ref[0]) + product(left_two_ref[...], right_two_ref[0])
    terms_ref[...] = total.astype(jnp.bfloat16).reshape(terms_ref.shape)


def pair_terms(left, right, chips):
    planes, tokens, columns = right.shape
    rows = left[0].shape[1] // chips
    group = max(1, 256 // rows)
    left_spec = pl.BlockSpec((tokens, group * rows), lambda p, m: (0, m))
    right_spec = pl.BlockSpec((1, tokens, columns), lambda p, m: (p, 0, 0))
    return pl.pallas_call(
        pair_kernel,
        grid=(planes, chips // group),
        in_specs=[left_spec, left_spec, right_spec, right_spec],
        out_specs=pl.BlockSpec(
            (group, 2, 1, rows // 2, columns), lambda p, m: (m, 0, p, 0, 0)
        ),
        out_shape=jax.ShapeDtypeStruct((chips, 2, planes, rows // 2, columns), jnp.bfloat16),
        cost_estimate=pl.CostEstimate(
            flops=4 * planes * tokens * chips * rows * columns,
            bytes_accessed=2 * planes * columns * (2 * tokens + chips * rows),
            transcendentals=0,
        ),
        name="pair_terms",
    )(left[0], left[1], right, partner(right))


SPAN = 128


def block_scores(queries, keys, starts_ref, block):
    rows = pl.ds(block * SPAN, SPAN)
    scores = lax.dot_general(
        queries, keys, (((1,), (1,)), ((), ())), preferred_element_type=jnp.float32
    ) * (HEAD_DIM ** (-0.5))
    query_pos = block * SPAN + lax.broadcasted_iota(jnp.int32, scores.shape, 0)
    key_pos = block * SPAN - WINDOW + lax.broadcasted_iota(jnp.int32, scores.shape, 1)
    mask = (
        (key_pos >= starts_ref[rows, :])
        & (key_pos <= query_pos)
        & (query_pos - key_pos < WINDOW)
    )
    scores = jnp.where(mask, scores, NEGATIVE)
    exponent = jnp.exp(scores - jnp.max(scores, axis=-1, keepdims=True))
    return exponent / jnp.sum(exponent, axis=-1, keepdims=True)


def attend_kernel(starts_ref, proj_ref, before_ref, mixed_ref):
    count = proj_ref.shape[1] // SPAN
    keys = jnp.concatenate([before_ref[0], proj_ref[1]], axis=0)
    values = jnp.concatenate([before_ref[1], proj_ref[2]], axis=0)
    for block in range(count):
        rows = slice(block * SPAN, (block + 1) * SPAN)
        seen = slice(block * SPAN, (block + 1) * SPAN + WINDOW)
        probs = block_scores(proj_ref[0, rows], keys[seen], starts_ref, block)
        mixed = jnp.dot(
            probs.astype(jnp.bfloat16), values[seen], preferred_element_type=jnp.float32
        )
        mixed_ref[rows, :] = mixed.astype(jnp.bfloat16)


def attend_back_kernel(
    starts_ref, proj_ref, before_ref, grad_ref, out_ref, rim_ref, tail_ref, keys_ref, values_ref
):
    count = proj_ref.shape[1] // SPAN
    scale = HEAD_DIM ** (-0.5)
    keys = jnp.concatenate([before_ref[0], proj_ref[1]], axis=0)
    values = jnp.concatenate([before_ref[1], proj_ref[2]], axis=0)
    keys_ref[...] = jnp.zeros_like(keys_ref)
    values_ref[...] = jnp.zeros_like(values_ref)

    def crossed(left, right):
        return lax.dot_general(
            left, right, (((0,), (0,)), ((), ())), preferred_element_type=jnp.float32
        )

    for block in range(count):
        rows = slice(block * SPAN, (block + 1) * SPAN)
        seen = slice(block * SPAN, (block + 1) * SPAN + WINDOW)
        queries = proj_ref[0, rows]
        grads = grad_ref[rows, :]
        probs = block_scores(queries, keys[seen], starts_ref, block)
        grad_probs = lax.dot_general(
            grads, values[seen], (((1,), (1,)), ((), ())), preferred_element_type=jnp.float32
        )
        inner = jnp.sum(probs * grad_probs, axis=-1, keepdims=True)
        grad_scores = (probs * (grad_probs - inner)).astype(jnp.bfloat16)
        grad_queries = jnp.dot(grad_scores, keys[seen], preferred_element_type=jnp.float32)
        out_ref[0, rows] = (grad_queries * scale).astype(jnp.bfloat16)
        keys_ref[seen, :] += crossed(grad_scores, queries) * scale
        values_ref[seen, :] += crossed(probs.astype(jnp.bfloat16), grads)
    tokens = count * SPAN
    for plane, total_ref in enumerate((keys_ref, values_ref)):
        rim_ref[plane] = total_ref[:WINDOW, :].astype(jnp.bfloat16)
        out_ref[1 + plane] = total_ref[WINDOW:, :].astype(jnp.bfloat16)
        tail_ref[plane] = total_ref[tokens:, :]


def attend(starts, proj, before):
    planes, tokens, width = proj.shape
    return pl.pallas_call(
        attend_kernel,
        grid=(width // HEAD_DIM,),
        in_specs=[
            pl.BlockSpec((tokens, 1), lambda h: (0, 0)),
            pl.BlockSpec((planes, tokens, HEAD_DIM), lambda h: (0, 0, h)),
            pl.BlockSpec((2, WINDOW, HEAD_DIM), lambda h: (0, 0, h)),
        ],
        out_specs=pl.BlockSpec((tokens, HEAD_DIM), lambda h: (0, h)),
        out_shape=jax.ShapeDtypeStruct((tokens, width), jnp.bfloat16),
        name="attend",
    )(starts, proj, before)


def attend_back(starts, proj, before, grad_mixed):
    planes, tokens, width = proj.shape
    rim_spec = pl.BlockSpec((2, WINDOW, HEAD_DIM), lambda h: (0, 0, h))
    proj_spec = pl.BlockSpec((planes, tokens, HEAD_DIM), lambda h: (0, 0, h))
    return pl.pallas_call(
        attend_back_kernel,
        grid=(width // HEAD_DIM,),
        in_specs=[
            pl.BlockSpec((tokens, 1), lambda h: (0, 0)),
            proj_spec,
            rim_spec,
            pl.BlockSpec((tokens, HEAD_DIM), lambda h: (0, h)),
        ],
        out_specs=[proj_spec, rim_spec, rim_spec],
        out_shape=[
            jax.ShapeDtypeStruct(proj.shape, jnp.bfloat16),
            jax.ShapeDtypeStruct((2, WINDOW, width), jnp.bfloat16),
            jax.ShapeDtypeStruct((2, WINDOW, width), jnp.float32),
        ],
        scratch_shapes=[pltpu.VMEM((tokens + WINDOW, HEAD_DIM), jnp.float32)] * 2,
        name="attend_back",
    )(starts, proj, before, grad_mixed)


def tp_sum(partial):
    sent = lax.optimization_barrier(partial.astype(jnp.bfloat16))
    other = lax.ppermute(sent, "tp", [(0, 1), (1, 0)])
    return sent.astype(jnp.float32) + other.astype(jnp.float32)


def gather_small(block):
    size = lax.axis_size("seq")
    index = lax.axis_index("seq")
    bit = 1
    while bit < size:
        other = lax.ppermute(block, "seq", [(i, i ^ bit) for i in range(size)])
        low_side = jnp.concatenate([block, other], axis=-1)
        high_side = jnp.concatenate([other, block], axis=-1)
        block = jnp.where(index & bit != 0, high_side, low_side)
        bit *= 2
    return block


def scatter_small(block):
    size = lax.axis_size("seq")
    index = lax.axis_index("seq")
    bit = size // 2
    while bit > 0:
        low_side, high_side = jnp.split(block, 2)
        upper = index & bit != 0
        given = jnp.where(upper, low_side, high_side)
        other = lax.ppermute(given, "seq", [(i, i ^ bit) for i in range(size)])
        block = jnp.where(upper, high_side, low_side) + other
        bit //= 2
    return block


def rms_scale(values_in, gain_vec):
    return (
        values_in
        * lax.rsqrt(jnp.mean(values_in * values_in, axis=-1, keepdims=True) + EPSILON)
        * gain_vec
    )


def gated(gate_part, up_part):
    return gate_part / (1.0 + jnp.exp(-gate_part)) * up_part


def doc_starts(lengths, positions):
    doc_ends = jnp.cumsum(lengths)
    return jnp.sum(jnp.where(doc_ends[None, :] <= positions[:, None], lengths[None, :], 0), axis=1)


def local(tokens, doc_lengths, gain_one, w_qkv, w_out, gain_two, w_gate_up, w_down, cotangent):
    token_count = tokens.shape[0]
    device = lax.axis_index("seq")
    chips = lax.axis_size("seq") // 2
    core = device % 2
    chip = device // 2
    place = jnp.where(chip % 2 == 0, chip // 2, chips - (chip + 1) // 2)
    row_length = token_count * lax.axis_size("seq") // doc_lengths.shape[0]
    first = (device * token_count) % row_length
    positions = first + jnp.arange(token_count, dtype=jnp.int32)
    starts = (doc_starts(doc_lengths[0], positions) - first).reshape(token_count, 1)
    f32 = jnp.float32
    bf16 = jnp.bfloat16

    gains = gather_small(jnp.stack([gain_one, gain_two])).astype(f32)
    gain_a = gains[0]
    gain_b = gains[1]
    first_weights = lax.all_gather(
        jnp.concatenate([w_qkv, w_out.T[:, None]], axis=1), "seq", axis=0, tiled=True
    )
    second_weights = lax.all_gather(
        jnp.concatenate([w_gate_up, w_down.T[:, None]], axis=1), "seq", axis=0, tiled=True
    )
    qkv_full = first_weights[:, :3]
    out_full = first_weights[:, 3]
    gate_up_full = second_weights[:, :2]
    down_full = second_weights[:, 2]

    token_rows = tokens.astype(f32)
    normed = rms_scale(token_rows, gain_a).astype(bf16)
    proj = jnp.einsum("td,dcf->ctf", normed, qkv_full, preferred_element_type=f32).astype(bf16)
    before = shifted(proj[1:, token_count - WINDOW :], "seq", 1)
    attn_mixed = attend(starts, proj, before)
    attn_out = tp_sum(jnp.einsum("tf,df->td", attn_mixed, out_full, preferred_element_type=f32))
    middle = token_rows + attn_out
    normed_two = rms_scale(middle, gain_b).astype(bf16)
    gate_up = jnp.einsum("td,dcf->ctf", normed_two, gate_up_full, preferred_element_type=f32)
    gate_part = gate_up[0]
    up_part = gate_up[1]
    hidden = gated(gate_part, up_part).astype(bf16)
    down_terms = pair_terms(pair_columns(cotangent, chips, core), hidden[None], chips)
    grad_w_down = ring_scatter(down_terms, chips, place)[0].T

    grad_hidden = jnp.einsum("td,df->tf", cotangent, down_full, preferred_element_type=f32)
    unused_value, gate_pull = jax.vjp(gated, gate_part, up_part)
    grad_gate_up = jnp.stack(gate_pull(grad_hidden)).astype(bf16)
    gate_up_terms = pair_terms(pair_columns(normed_two, chips, core), grad_gate_up, chips)
    grad_w_gate_up = ring_scatter(gate_up_terms, chips, place).transpose(1, 0, 2)
    grad_normed_two = tp_sum(
        jnp.einsum("ctf,dcf->td", grad_gate_up, gate_up_full, preferred_element_type=f32)
    )
    branch = tp_sum(jnp.einsum("tf,df->td", hidden, down_full, preferred_element_type=f32))
    result = (middle + branch).astype(bf16)

    unused_norm, norm_pull = jax.vjp(rms_scale, middle, gain_b)
    grad_mid_norm, grad_gain_two = norm_pull(grad_normed_two)
    grad_middle = cotangent.astype(f32) + grad_mid_norm
    grad_gain_two = scatter_small(grad_gain_two)
    grad_attn = grad_middle.astype(bf16)
    grad_mixed = jnp.einsum("td,df->tf", grad_attn, out_full, preferred_element_type=f32).astype(
        bf16
    )
    out_terms = pair_terms(pair_columns(grad_attn, chips, core), attn_mixed[None], chips)
    grad_w_out = ring_scatter(out_terms, chips, place)[0].T

    grad_proj, rim, tail = attend_back(starts, proj, before, grad_mixed)
    arrived = shifted(rim, "seq", -1).astype(f32)
    grad_proj = grad_proj.at[1:, token_count - WINDOW :].set((tail + arrived).astype(bf16))
    qkv_terms = pair_terms(pair_columns(normed, chips, core), grad_proj, chips)
    grad_w_qkv = ring_scatter(qkv_terms, chips, place).transpose(1, 0, 2)
    grad_normed = tp_sum(
        jnp.einsum("ctf,dcf->td", grad_proj, qkv_full, preferred_element_type=f32)
    )
    unused_first, first_pull = jax.vjp(rms_scale, token_rows, gain_a)
    grad_rows_norm, grad_gain_one = first_pull(grad_normed)
    grad_tokens = grad_middle + grad_rows_norm
    grad_gain_one = scatter_small(grad_gain_one)
    return (
        result,
        grad_tokens,
        grad_gain_one,
        grad_w_qkv,
        grad_w_out,
        grad_gain_two,
        grad_w_gate_up,
        grad_w_down,
    )


def solution(mesh):
    return jax.shard_map(
        local,
        mesh=mesh,
        in_specs=(
            P("seq", None),
            P(),
            P("seq"),
            P("seq", None, "tp"),
            P("tp", "seq"),
            P("seq"),
            P("seq", None, "tp"),
            P("tp", "seq"),
            P("seq", None),
        ),
        out_specs=(
            P("seq", None),
            P("seq", None),
            P("seq"),
            P("seq", None, "tp"),
            P("tp", "seq"),
            P("seq"),
            P("seq", None, "tp"),
            P("tp", "seq"),
        ),
        check_vma=False,
    )
```

```python
import jax
import jax.numpy as jnp
from jax import lax
from jax.experimental import pallas as pl
from jax.experimental.pallas import tpu as pltpu
from jax.sharding import PartitionSpec as P

HEAD_DIM = 128
WINDOW = 64


EPSILON = 1e-05
NEGATIVE = -1e30


def shifted(block, axis, distance):
    devices = range(lax.axis_size(axis))
    route = [(i - distance, i) for i in devices if i - distance in devices]
    return lax.ppermute(block, axis, route)


def chip_at(place, chips):
    place = place % chips
    return jnp.where(place < chips // 2, 2 * place, 2 * chips - 1 - 2 * place)


def ring_routes(chips):
    cycle = list(range(0, chips, 2)) + list(range(1, chips, 2))[::-1]
    ahead = []
    for place in range(chips):
        for core in range(2):
            ahead.append((2 * cycle[place] + core, 2 * cycle[(place + 1) % chips] + core))
    return ahead, [(target, source) for source, target in ahead]


class Ring:
    def __init__(self, terms, chips, place):
        self.terms = terms
        self.chips = chips
        self.place = place
        self.hop = 1
        self.routes = ring_routes(chips)
        self.sums = [self.part(direction) for direction in range(2)]

    def part(self, direction):
        chip = chip_at(self.place - (1, -1)[direction] * self.hop, self.chips)
        start = (chip, direction, 0, 0, 0)
        return lax.dynamic_slice(self.terms, start, (1, 1) + self.terms.shape[2:])[0, 0]

    def open(self):
        return self.hop < self.chips

    def send(self):
        return [lax.ppermute(self.sums[d], "seq", self.routes[d]) for d in range(2)]

    def take(self, arrived):
        self.hop += 1
        for direction in range(2):
            total = arrived[direction].astype(jnp.float32)
            total = total + self.part(direction).astype(jnp.float32)
            self.sums[direction] = total if not self.open() else total.astype(jnp.bfloat16)

    def result(self):
        while self.open():
            self.take(self.send())
        return jnp.concatenate(self.sums, axis=1)


def beside(rings, work, *given):
    rings = [ring for ring in rings if ring.open()]
    sums, given = lax.optimization_barrier(([ring.sums for ring in rings], given))
    for ring, held in zip(rings, sums):
        ring.sums = held
    arrived = [ring.send() for ring in rings]
    made = work(*given)
    arrived, made = lax.optimization_barrier((arrived, made))
    for ring, blocks in zip(rings, arrived):
        ring.take(blocks)
    return made


def partner(block):
    size = lax.axis_size("seq")
    return lax.ppermute(block, "seq", [(i, i ^ 1) for i in range(size)])


def select_kernel(core_ref, block_ref, kept_ref, given_ref):
    rows = 128
    for chip in range(kept_ref.shape[1] // rows):
        even = block_ref[:, 2 * chip * rows : (2 * chip + 1) * rows]
        odd = block_ref[:, (2 * chip + 1) * rows : (2 * chip + 2) * rows]
        first = core_ref[0] == 0
        kept_ref[:, chip * rows : (chip + 1) * rows] = jnp.where(first, even, odd)
        given_ref[:, chip * rows : (chip + 1) * rows] = jnp.where(first, odd, even)


def pair_columns(block, chips, core):
    tokens, width = block.shape
    rows = width // (2 * chips)
    half = jax.ShapeDtypeStruct((tokens, width // 2), block.dtype)
    if rows == 128:
        group = 128
        kept, given = pl.pallas_call(
            select_kernel,
            grid_spec=pltpu.PrefetchScalarGridSpec(
                num_scalar_prefetch=1,
                grid=(tokens // group,),
                in_specs=[pl.BlockSpec((group, width), lambda t, c: (t, 0))],
                out_specs=[pl.BlockSpec((group, width // 2), lambda t, c: (t, 0))] * 2,
            ),
            out_shape=[half, half],
            name="select_columns",
        )(core.reshape(1), block)
    else:
        split = block.reshape(tokens, chips, 2, rows)
        kept = lax.dynamic_index_in_dim(split, core, 2, keepdims=False).reshape(half.shape)
        given = lax.dynamic_index_in_dim(split, 1 - core, 2, keepdims=False).reshape(half.shape)
    return kept, partner(given)


def pair_kernel(left_ref, left_two_ref, right_ref, right_two_ref, terms_ref):
    def product(left, right):
        return lax.dot_general(
            left, right, (((0,), (0,)), ((), ())), preferred_element_type=jnp.float32
        )

    total = product(left_ref[...], right_ref[0]) + product(left_two_ref[...], right_two_ref[0])
    terms_ref[...] = total.astype(jnp.bfloat16).reshape(terms_ref.shape)


def pair_terms(left, right, right_two, chips):
    planes, tokens, columns = right.shape
    rows = left[0].shape[1] // chips
    group = max(1, 256 // rows)
    left_spec = pl.BlockSpec((tokens, group * rows), lambda p, m: (0, m))
    right_spec = pl.BlockSpec((1, tokens, columns), lambda p, m: (p, 0, 0))
    return pl.pallas_call(
        pair_kernel,
        grid=(planes, chips // group),
        in_specs=[left_spec, left_spec, right_spec, right_spec],
        out_specs=pl.BlockSpec(
            (group, 2, 1, rows // 2, columns), lambda p, m: (m, 0, p, 0, 0)
        ),
        out_shape=jax.ShapeDtypeStruct((chips, 2, planes, rows // 2, columns), jnp.bfloat16),
        cost_estimate=pl.CostEstimate(
            flops=4 * planes * tokens * chips * rows * columns,
            bytes_accessed=2 * planes * columns * (2 * tokens + chips * rows),
            transcendentals=0,
        ),
        name="pair_terms",
    )(left[0], left[1], right, right_two)


SPAN = 128


def block_scores(queries, keys, starts_ref, block):
    rows = pl.ds(block * SPAN, SPAN)
    scores = lax.dot_general(
        queries, keys, (((1,), (1,)), ((), ())), preferred_element_type=jnp.float32
    ) * (HEAD_DIM ** (-0.5))
    query_pos = block * SPAN + lax.broadcasted_iota(jnp.int32, scores.shape, 0)
    key_pos = block * SPAN - WINDOW + lax.broadcasted_iota(jnp.int32, scores.shape, 1)
    mask = (
        (key_pos >= starts_ref[rows, :])
        & (key_pos <= query_pos)
        & (query_pos - key_pos < WINDOW)
    )
    scores = jnp.where(mask, scores, NEGATIVE)
    exponent = jnp.exp(scores - jnp.max(scores, axis=-1, keepdims=True))
    return exponent / jnp.sum(exponent, axis=-1, keepdims=True)


def attend_kernel(starts_ref, proj_ref, before_ref, mixed_ref):
    count = proj_ref.shape[1] // SPAN
    keys = jnp.concatenate([before_ref[0], proj_ref[1]], axis=0)
    values = jnp.concatenate([before_ref[1], proj_ref[2]], axis=0)
    for block in range(count):
        rows = slice(block * SPAN, (block + 1) * SPAN)
        seen = slice(block * SPAN, (block + 1) * SPAN + WINDOW)
        probs = block_scores(proj_ref[0, rows], keys[seen], starts_ref, block)
        mixed = jnp.dot(
            probs.astype(jnp.bfloat16), values[seen], preferred_element_type=jnp.float32
        )
        mixed_ref[rows, :] = mixed.astype(jnp.bfloat16)


def attend_back_kernel(
    starts_ref, proj_ref, before_ref, grad_ref, out_ref, rim_ref, tail_ref, keys_ref, values_ref
):
    count = proj_ref.shape[1] // SPAN
    scale = HEAD_DIM ** (-0.5)
    keys = jnp.concatenate([before_ref[0], proj_ref[1]], axis=0)
    values = jnp.concatenate([before_ref[1], proj_ref[2]], axis=0)
    keys_ref[...] = jnp.zeros_like(keys_ref)
    values_ref[...] = jnp.zeros_like(values_ref)

    def crossed(left, right):
        return lax.dot_general(
            left, right, (((0,), (0,)), ((), ())), preferred_element_type=jnp.float32
        )

    for block in range(count):
        rows = slice(block * SPAN, (block + 1) * SPAN)
        seen = slice(block * SPAN, (block + 1) * SPAN + WINDOW)
        queries = proj_ref[0, rows]
        grads = grad_ref[rows, :]
        probs = block_scores(queries, keys[seen], starts_ref, block)
        grad_probs = lax.dot_general(
            grads, values[seen], (((1,), (1,)), ((), ())), preferred_element_type=jnp.float32
        )
        inner = jnp.sum(probs * grad_probs, axis=-1, keepdims=True)
        grad_scores = (probs * (grad_probs - inner)).astype(jnp.bfloat16)
        grad_queries = jnp.dot(grad_scores, keys[seen], preferred_element_type=jnp.float32)
        out_ref[0, rows] = (grad_queries * scale).astype(jnp.bfloat16)
        keys_ref[seen, :] += crossed(grad_scores, queries) * scale
        values_ref[seen, :] += crossed(probs.astype(jnp.bfloat16), grads)
    tokens = count * SPAN
    for plane, total_ref in enumerate((keys_ref, values_ref)):
        rim_ref[plane] = total_ref[:WINDOW, :].astype(jnp.bfloat16)
        out_ref[1 + plane] = total_ref[WINDOW:, :].astype(jnp.bfloat16)
        tail_ref[plane] = total_ref[tokens:, :]


def attend(starts, proj, before):
    planes, tokens, width = proj.shape
    return pl.pallas_call(
        attend_kernel,
        grid=(width // HEAD_DIM,),
        in_specs=[
            pl.BlockSpec((tokens, 1), lambda h: (0, 0)),
            pl.BlockSpec((planes, tokens, HEAD_DIM), lambda h: (0, 0, h)),
            pl.BlockSpec((2, WINDOW, HEAD_DIM), lambda h: (0, 0, h)),
        ],
        out_specs=pl.BlockSpec((tokens, HEAD_DIM), lambda h: (0, h)),
        out_shape=jax.ShapeDtypeStruct((tokens, width), jnp.bfloat16),
        name="attend",
    )(starts, proj, before)


def attend_back(starts, proj, before, grad_mixed):
    planes, tokens, width = proj.shape
    rim_spec = pl.BlockSpec((2, WINDOW, HEAD_DIM), lambda h: (0, 0, h))
    proj_spec = pl.BlockSpec((planes, tokens, HEAD_DIM), lambda h: (0, 0, h))
    return pl.pallas_call(
        attend_back_kernel,
        grid=(width // HEAD_DIM,),
        in_specs=[
            pl.BlockSpec((tokens, 1), lambda h: (0, 0)),
            proj_spec,
            rim_spec,
            pl.BlockSpec((tokens, HEAD_DIM), lambda h: (0, h)),
        ],
        out_specs=[proj_spec, rim_spec, rim_spec],
        out_shape=[
            jax.ShapeDtypeStruct(proj.shape, jnp.bfloat16),
            jax.ShapeDtypeStruct((2, WINDOW, width), jnp.bfloat16),
            jax.ShapeDtypeStruct((2, WINDOW, width), jnp.float32),
        ],
        scratch_shapes=[pltpu.VMEM((tokens + WINDOW, HEAD_DIM), jnp.float32)] * 2,
        name="attend_back",
    )(starts, proj, before, grad_mixed)


def tp_send(sent):
    return sent.astype(jnp.float32) + lax.ppermute(sent, "tp", [(0, 1), (1, 0)]).astype(jnp.float32)


def tp_sum(partial):
    return tp_send(lax.optimization_barrier(partial.astype(jnp.bfloat16)))


def gather_small(block):
    size = lax.axis_size("seq")
    index = lax.axis_index("seq")
    bit = 1
    while bit < size:
        other = lax.ppermute(block, "seq", [(i, i ^ bit) for i in range(size)])
        low_side = jnp.concatenate([block, other], axis=-1)
        high_side = jnp.concatenate([other, block], axis=-1)
        block = jnp.where(index & bit != 0, high_side, low_side)
        bit *= 2
    return block


def scatter_small(block):
    size = lax.axis_size("seq")
    index = lax.axis_index("seq")
    bit = size // 2
    while bit > 0:
        low_side, high_side = jnp.split(block, 2)
        upper = index & bit != 0
        given = jnp.where(upper, low_side, high_side)
        other = lax.ppermute(given, "seq", [(i, i ^ bit) for i in range(size)])
        block = jnp.where(upper, high_side, low_side) + other
        bit //= 2
    return block


def rms_scale(values_in, gain_vec):
    return (
        values_in
        * lax.rsqrt(jnp.mean(values_in * values_in, axis=-1, keepdims=True) + EPSILON)
        * gain_vec
    )


def gated(gate_part, up_part):
    return gate_part / (1.0 + jnp.exp(-gate_part)) * up_part


def doc_starts(lengths, positions):
    doc_ends = jnp.cumsum(lengths)
    return jnp.sum(jnp.where(doc_ends[None, :] <= positions[:, None], lengths[None, :], 0), axis=1)


def local(tokens, doc_lengths, gain_one, w_qkv, w_out, gain_two, w_gate_up, w_down, cotangent):
    token_count = tokens.shape[0]
    device = lax.axis_index("seq")
    chips = lax.axis_size("seq") // 2
    core = device % 2
    chip = device // 2
    place = jnp.where(chip % 2 == 0, chip // 2, chips - (chip + 1) // 2)
    row_length = token_count * lax.axis_size("seq") // doc_lengths.shape[0]
    first = (device * token_count) % row_length
    positions = first + jnp.arange(token_count, dtype=jnp.int32)
    starts = (doc_starts(doc_lengths[0], positions) - first).reshape(token_count, 1)
    f32 = jnp.float32
    bf16 = jnp.bfloat16

    first_own = jnp.concatenate([w_qkv, w_out.T[:, None]], axis=1)
    second_own = jnp.concatenate([w_gate_up, w_down.T[:, None]], axis=1)
    gains = jnp.stack([gain_one, gain_two])
    first_own, second_own, gains = lax.optimization_barrier((first_own, second_own, gains))
    first_weights = lax.all_gather(first_own, "seq", axis=0, tiled=True)
    second_weights = lax.all_gather(second_own, "seq", axis=0, tiled=True)
    gains = gather_small(gains).astype(f32)
    gain_a = gains[0]
    gain_b = gains[1]
    qkv_full = first_weights[:, :3]
    out_full = first_weights[:, 3]
    gate_up_full = second_weights[:, :2]
    down_full = second_weights[:, 2]

    token_rows = tokens.astype(f32)
    normed = rms_scale(token_rows, gain_a).astype(bf16)
    proj = jnp.einsum("td,dcf->ctf", normed, qkv_full, preferred_element_type=f32).astype(bf16)
    before = shifted(proj[1:, token_count - WINDOW :], "seq", 1)
    attn_mixed = attend(starts, proj, before)
    attn_out = tp_sum(jnp.einsum("tf,df->td", attn_mixed, out_full, preferred_element_type=f32))
    middle = token_rows + attn_out
    normed_two = rms_scale(middle, gain_b).astype(bf16)
    gate_up = jnp.einsum("td,dcf->ctf", normed_two, gate_up_full, preferred_element_type=f32)
    hidden = gated(gate_up[0], gate_up[1]).astype(bf16)
    cot_pair = pair_columns(cotangent, chips, core)
    normed_two_pair = pair_columns(normed_two, chips, core)
    normed_pair = pair_columns(normed, chips, core)
    hidden, cot_held = lax.optimization_barrier((hidden, cotangent))
    hidden_two = partner(hidden[None])
    grad_hidden = jnp.einsum("td,df->tf", cot_held, down_full, preferred_element_type=f32)
    down_terms = pair_terms(cot_pair, hidden[None], hidden_two, chips)
    down = Ring(down_terms, chips, place)

    def through_gate(grad_hidden, gate_up):
        unused_value, gate_pull = jax.vjp(gated, gate_up[0], gate_up[1])
        return jnp.stack(gate_pull(grad_hidden)).astype(bf16)

    grad_gate_up = beside([down], through_gate, grad_hidden, gate_up)
    grad_gate_up_two = partner(grad_gate_up)

    def through_gate_up(grad_gate_up):
        return jnp.einsum(
            "ctf,dcf->td", grad_gate_up, gate_up_full, preferred_element_type=f32
        ).astype(bf16)

    sent_two = beside([down], through_gate_up, grad_gate_up)
    grad_normed_two = tp_send(sent_two)

    def gate_up_product(grad_gate_up):
        return pair_terms(normed_two_pair, grad_gate_up, grad_gate_up_two, chips)

    gate_up_ring = Ring(beside([down], gate_up_product, grad_gate_up), chips, place)

    def through_down(hidden):
        return jnp.einsum("tf,df->td", hidden, down_full, preferred_element_type=f32).astype(bf16)

    rings = [down, gate_up_ring]
    branch = tp_send(beside(rings, through_down, hidden))

    def through_norm_two(middle):
        unused_norm, norm_pull = jax.vjp(rms_scale, middle, gain_b)
        grad_mid_norm, grad_gain_two = norm_pull(grad_normed_two)
        grad_middle = cotangent.astype(f32) + grad_mid_norm
        grad_attn = grad_middle.astype(bf16)
        grad_mixed = jnp.einsum("td,df->tf", grad_attn, out_full, preferred_element_type=f32)
        return grad_middle, grad_gain_two, grad_attn, grad_mixed.astype(bf16)

    grad_middle, grad_gain_two, grad_attn, grad_mixed = beside(rings, through_norm_two, middle)
    grad_gain_two = scatter_small(grad_gain_two)
    mixed_two = partner(attn_mixed[None])
    grad_attn_pair = pair_columns(grad_attn, chips, core)

    def through_attention(grad_mixed):
        return attend_back(starts, proj, before, grad_mixed)

    grad_proj, rim, tail = beside(rings, through_attention, grad_mixed)
    arrived = shifted(rim, "seq", -1).astype(f32)

    def out_product(grad_proj):
        out_terms = pair_terms(grad_attn_pair, attn_mixed[None], mixed_two, chips)
        edge = (tail + arrived).astype(bf16)
        return out_terms, grad_proj.at[1:, token_count - WINDOW :].set(edge)

    out_terms, grad_proj = beside(rings, out_product, grad_proj)
    rings.append(Ring(out_terms, chips, place))
    grad_proj_two = partner(grad_proj)

    def through_qkv(grad_proj):
        return jnp.einsum(
            "ctf,dcf->td", grad_proj, qkv_full, preferred_element_type=f32
        ).astype(bf16)

    grad_normed = tp_send(beside(rings, through_qkv, grad_proj))

    def qkv_product(grad_proj):
        return pair_terms(normed_pair, grad_proj, grad_proj_two, chips)

    rings.append(Ring(beside(rings, qkv_product, grad_proj), chips, place))

    def finish(middle):
        return (middle + branch).astype(bf16), down.result()[0].T

    result, grad_w_down = beside(rings, finish, middle)

    def finish_gate_up(whole):
        return whole.transpose(1, 0, 2)

    grad_w_gate_up = beside(rings, finish_gate_up, gate_up_ring.result())

    def through_norm(token_rows):
        unused_first, first_pull = jax.vjp(rms_scale, token_rows, gain_a)
        grad_rows_norm, grad_gain_one = first_pull(grad_normed)
        return grad_middle + grad_rows_norm, grad_gain_one

    grad_tokens, grad_gain_one = beside(rings, through_norm, token_rows)
    grad_gain_one = scatter_small(grad_gain_one)
    grad_w_out = rings[2].result()[0].T
    grad_w_qkv = rings[3].result().transpose(1, 0, 2)
    return (
        result,
        grad_tokens,
        grad_gain_one,
        grad_w_qkv,
        grad_w_out,
        grad_gain_two,
        grad_w_gate_up,
        grad_w_down,
    )


def solution(mesh):
    return jax.shard_map(
        local,
        mesh=mesh,
        in_specs=(
            P("seq", None),
            P(),
            P("seq"),
            P("seq", None, "tp"),
            P("tp", "seq"),
            P("seq"),
            P("seq", None, "tp"),
            P("tp", "seq"),
            P("seq", None),
        ),
        out_specs=(
            P("seq", None),
            P("seq", None),
            P("seq"),
            P("seq", None, "tp"),
            P("tp", "seq"),
            P("seq"),
            P("seq", None, "tp"),
            P("tp", "seq"),
        ),
        check_vma=False,
    )
```

```python
import jax
import jax.numpy as jnp
from jax import lax
from jax.experimental import pallas as pl
from jax.experimental.layout import Layout, with_layout_constraint
from jax.experimental.pallas import tpu as pltpu
from jax.sharding import PartitionSpec as P

HEAD_DIM = 128
WINDOW = 64


EPSILON = 1e-05
NEGATIVE = -1e30


def shifted(block, axis, distance):
    devices = range(lax.axis_size(axis))
    route = [(i - distance, i) for i in devices if i - distance in devices]
    return lax.ppermute(block, axis, route)


def chip_at(place, chips):
    place = place % chips
    return jnp.where(place < chips // 2, 2 * place, 2 * chips - 1 - 2 * place)


def ring_routes(chips):
    cycle = list(range(0, chips, 2)) + list(range(1, chips, 2))[::-1]
    ahead = []
    for place in range(chips):
        for core in range(2):
            ahead.append((2 * cycle[place] + core, 2 * cycle[(place + 1) % chips] + core))
    return ahead, [(target, source) for source, target in ahead]


class Ring:
    def __init__(self, terms, chips, place):
        self.terms = terms
        self.chips = chips
        self.place = place
        self.hop = 1
        self.routes = ring_routes(chips)
        self.sums = [self.part(direction) for direction in range(2)]

    def part(self, direction):
        chip = chip_at(self.place - (1, -1)[direction] * self.hop, self.chips)
        start = (chip, direction, 0, 0, 0)
        return lax.dynamic_slice(self.terms, start, (1, 1) + self.terms.shape[2:])[0, 0]

    def open(self):
        return self.hop < self.chips

    def send(self):
        return [lax.ppermute(self.sums[d], "seq", self.routes[d]) for d in range(2)]

    def take(self, arrived):
        self.hop += 1
        for direction in range(2):
            total = arrived[direction].astype(jnp.float32)
            total = total + self.part(direction).astype(jnp.float32)
            self.sums[direction] = total if not self.open() else total.astype(jnp.bfloat16)

    def result(self):
        while self.open():
            self.take(self.send())
        return jnp.concatenate(self.sums, axis=1)


def beside(rings, extra, work, *given):
    rings = [ring for ring in rings if ring.open()]
    sums, blocks, given = lax.optimization_barrier(
        ([ring.sums for ring in rings], [block for block, axis, route in extra], given)
    )
    for ring, held in zip(rings, sums):
        ring.sums = held
    arrived = [ring.send() for ring in rings]
    others = [
        lax.ppermute(block, axis, route) for block, (held, axis, route) in zip(blocks, extra)
    ]
    made = work(*given)
    arrived, others, made = lax.optimization_barrier((arrived, others, made))
    for ring, sums in zip(rings, arrived):
        ring.take(sums)
    return made, others


def row_major(block):
    return with_layout_constraint(block, Layout(major_to_minor=tuple(range(block.ndim))))


def to_partner(block):
    size = lax.axis_size("seq")
    return (row_major(block), "seq", [(i, i ^ 1) for i in range(size)])


def tp_rows(block, first, last):
    tokens = block.shape[0]
    part = block[first * tokens // 4 : last * tokens // 4]
    return (part, "tp", [(0, 1), (1, 0)])


def tp_join(block, parts):
    return block.astype(jnp.float32) + jnp.concatenate(parts).astype(jnp.float32)


def partner(block):
    size = lax.axis_size("seq")
    return lax.ppermute(block, "seq", [(i, i ^ 1) for i in range(size)])


def select_kernel(core_ref, block_ref, kept_ref, given_ref):
    rows = 128
    for chip in range(kept_ref.shape[1] // rows):
        even = block_ref[:, 2 * chip * rows : (2 * chip + 1) * rows]
        odd = block_ref[:, (2 * chip + 1) * rows : (2 * chip + 2) * rows]
        first = core_ref[0] == 0
        kept_ref[:, chip * rows : (chip + 1) * rows] = jnp.where(first, even, odd)
        given_ref[:, chip * rows : (chip + 1) * rows] = jnp.where(first, odd, even)


def pair_columns(block, chips, core):
    tokens, width = block.shape
    rows = width // (2 * chips)
    half = jax.ShapeDtypeStruct((tokens, width // 2), block.dtype)
    if rows == 128:
        group = 128
        kept, given = pl.pallas_call(
            select_kernel,
            grid_spec=pltpu.PrefetchScalarGridSpec(
                num_scalar_prefetch=1,
                grid=(tokens // group,),
                in_specs=[pl.BlockSpec((group, width), lambda t, c: (t, 0))],
                out_specs=[pl.BlockSpec((group, width // 2), lambda t, c: (t, 0))] * 2,
            ),
            out_shape=[half, half],
            name="select_columns",
        )(core.reshape(1), block)
    else:
        split = block.reshape(tokens, chips, 2, rows)
        kept = lax.dynamic_index_in_dim(split, core, 2, keepdims=False).reshape(half.shape)
        given = lax.dynamic_index_in_dim(split, 1 - core, 2, keepdims=False).reshape(half.shape)
    return kept, partner(given)


def pair_kernel(left_ref, left_two_ref, right_ref, right_two_ref, terms_ref):
    def product(left, right):
        return lax.dot_general(
            left, right, (((0,), (0,)), ((), ())), preferred_element_type=jnp.float32
        )

    total = product(left_ref[...], right_ref[0]) + product(left_two_ref[...], right_two_ref[0])
    terms_ref[...] = total.astype(jnp.bfloat16).reshape(terms_ref.shape)


def pair_terms(left, right, right_two, chips):
    planes, tokens, columns = right.shape
    rows = left[0].shape[1] // chips
    group = max(1, 256 // rows)
    left_spec = pl.BlockSpec((tokens, group * rows), lambda p, m: (0, m))
    right_spec = pl.BlockSpec((1, tokens, columns), lambda p, m: (p, 0, 0))
    return pl.pallas_call(
        pair_kernel,
        grid=(planes, chips // group),
        in_specs=[left_spec, left_spec, right_spec, right_spec],
        out_specs=pl.BlockSpec(
            (group, 2, 1, rows // 2, columns), lambda p, m: (m, 0, p, 0, 0)
        ),
        out_shape=jax.ShapeDtypeStruct((chips, 2, planes, rows // 2, columns), jnp.bfloat16),
        cost_estimate=pl.CostEstimate(
            flops=4 * planes * tokens * chips * rows * columns,
            bytes_accessed=2 * planes * columns * (2 * tokens + chips * rows),
            transcendentals=0,
        ),
        name="pair_terms",
    )(left[0], left[1], right, right_two)


SPAN = 128


def block_scores(queries, keys, starts_ref, block):
    rows = pl.ds(block * SPAN, SPAN)
    scores = lax.dot_general(
        queries, keys, (((1,), (1,)), ((), ())), preferred_element_type=jnp.float32
    ) * (HEAD_DIM ** (-0.5))
    query_pos = block * SPAN + lax.broadcasted_iota(jnp.int32, scores.shape, 0)
    key_pos = block * SPAN - WINDOW + lax.broadcasted_iota(jnp.int32, scores.shape, 1)
    mask = (
        (key_pos >= starts_ref[rows, :])
        & (key_pos <= query_pos)
        & (query_pos - key_pos < WINDOW)
    )
    scores = jnp.where(mask, scores, NEGATIVE)
    exponent = jnp.exp(scores - jnp.max(scores, axis=-1, keepdims=True))
    return exponent / jnp.sum(exponent, axis=-1, keepdims=True)


def attend_kernel(starts_ref, queries_ref, keys_ref, values_ref, before_ref, mixed_ref):
    count = queries_ref.shape[0] // SPAN
    keys = jnp.concatenate([before_ref[0], keys_ref[...]], axis=0)
    values = jnp.concatenate([before_ref[1], values_ref[...]], axis=0)
    for block in range(count):
        rows = slice(block * SPAN, (block + 1) * SPAN)
        seen = slice(block * SPAN, (block + 1) * SPAN + WINDOW)
        probs = block_scores(queries_ref[rows, :], keys[seen], starts_ref, block)
        mixed = jnp.dot(
            probs.astype(jnp.bfloat16), values[seen], preferred_element_type=jnp.float32
        )
        mixed_ref[rows, :] = mixed.astype(jnp.bfloat16)


def attend_back_kernel(
    starts_ref,
    queries_ref,
    keys_ref,
    values_ref,
    before_ref,
    grad_ref,
    grad_queries_ref,
    grad_keys_ref,
    grad_values_ref,
    rim_ref,
    tail_ref,
    key_sum_ref,
    value_sum_ref,
):
    count = queries_ref.shape[0] // SPAN
    scale = HEAD_DIM ** (-0.5)
    keys = jnp.concatenate([before_ref[0], keys_ref[...]], axis=0)
    values = jnp.concatenate([before_ref[1], values_ref[...]], axis=0)
    key_sum_ref[...] = jnp.zeros_like(key_sum_ref)
    value_sum_ref[...] = jnp.zeros_like(value_sum_ref)

    def crossed(left, right):
        return lax.dot_general(
            left, right, (((0,), (0,)), ((), ())), preferred_element_type=jnp.float32
        )

    for block in range(count):
        rows = slice(block * SPAN, (block + 1) * SPAN)
        seen = slice(block * SPAN, (block + 1) * SPAN + WINDOW)
        queries = queries_ref[rows, :]
        grads = grad_ref[rows, :]
        probs = block_scores(queries, keys[seen], starts_ref, block)
        grad_probs = lax.dot_general(
            grads, values[seen], (((1,), (1,)), ((), ())), preferred_element_type=jnp.float32
        )
        inner = jnp.sum(probs * grad_probs, axis=-1, keepdims=True)
        grad_scores = (probs * (grad_probs - inner)).astype(jnp.bfloat16)
        grad_queries = jnp.dot(grad_scores, keys[seen], preferred_element_type=jnp.float32)
        grad_queries_ref[rows, :] = (grad_queries * scale).astype(jnp.bfloat16)
        key_sum_ref[seen, :] += crossed(grad_scores, queries) * scale
        value_sum_ref[seen, :] += crossed(probs.astype(jnp.bfloat16), grads)
    tokens = count * SPAN
    totals = ((key_sum_ref, grad_keys_ref), (value_sum_ref, grad_values_ref))
    for plane, (total_ref, out_ref) in enumerate(totals):
        rim_ref[plane] = total_ref[:WINDOW, :].astype(jnp.bfloat16)
        out_ref[...] = total_ref[WINDOW:, :].astype(jnp.bfloat16)
        tail_ref[plane] = total_ref[tokens:, :]


def head_specs(tokens, heads):
    starts_spec = pl.BlockSpec((tokens, 1), lambda h: (0, 0))
    part_specs = [
        pl.BlockSpec((tokens, HEAD_DIM), lambda h, part=part: (0, part * heads + h))
        for part in range(3)
    ]
    rim_spec = pl.BlockSpec((2, WINDOW, HEAD_DIM), lambda h: (0, 0, h))
    return starts_spec, part_specs, rim_spec


def attend(starts, proj, before):
    tokens, width = proj.shape[0], proj.shape[1] // 3
    heads = width // HEAD_DIM
    starts_spec, part_specs, rim_spec = head_specs(tokens, heads)
    return pl.pallas_call(
        attend_kernel,
        grid=(heads,),
        in_specs=[starts_spec, *part_specs, rim_spec],
        out_specs=part_specs[0],
        out_shape=jax.ShapeDtypeStruct((tokens, width), jnp.bfloat16),
        name="attend",
    )(starts, proj, proj, proj, before)


def attend_back(starts, proj, before, grad_mixed):
    tokens, width = grad_mixed.shape
    heads = width // HEAD_DIM
    starts_spec, part_specs, rim_spec = head_specs(tokens, heads)
    whole = jax.ShapeDtypeStruct((tokens, width), jnp.bfloat16)
    return pl.pallas_call(
        attend_back_kernel,
        grid=(heads,),
        in_specs=[starts_spec, *part_specs, rim_spec, part_specs[0]],
        out_specs=[part_specs[0]] * 3 + [rim_spec] * 2,
        out_shape=[whole] * 3
        + [
            jax.ShapeDtypeStruct((2, WINDOW, width), jnp.bfloat16),
            jax.ShapeDtypeStruct((2, WINDOW, width), jnp.float32),
        ],
        scratch_shapes=[pltpu.VMEM((tokens + WINDOW, HEAD_DIM), jnp.float32)] * 2,
        name="attend_back",
    )(starts, proj, proj, proj, before, grad_mixed)


def tp_send(sent):
    return sent.astype(jnp.float32) + lax.ppermute(sent, "tp", [(0, 1), (1, 0)]).astype(jnp.float32)


def tp_sum(partial):
    return tp_send(lax.optimization_barrier(partial.astype(jnp.bfloat16)))


def gather_small(block):
    size = lax.axis_size("seq")
    index = lax.axis_index("seq")
    bit = 1
    while bit < size:
        other = lax.ppermute(block, "seq", [(i, i ^ bit) for i in range(size)])
        low_side = jnp.concatenate([block, other], axis=-1)
        high_side = jnp.concatenate([other, block], axis=-1)
        block = jnp.where(index & bit != 0, high_side, low_side)
        bit *= 2
    return block


def scatter_small(block):
    size = lax.axis_size("seq")
    index = lax.axis_index("seq")
    bit = size // 2
    while bit > 0:
        low_side, high_side = jnp.split(block, 2)
        upper = index & bit != 0
        given = jnp.where(upper, low_side, high_side)
        other = lax.ppermute(given, "seq", [(i, i ^ bit) for i in range(size)])
        block = jnp.where(upper, high_side, low_side) + other
        bit //= 2
    return block


def rms_scale(values_in, gain_vec):
    return (
        values_in
        * lax.rsqrt(jnp.mean(values_in * values_in, axis=-1, keepdims=True) + EPSILON)
        * gain_vec
    )


def gated(gate_part, up_part):
    return gate_part / (1.0 + jnp.exp(-gate_part)) * up_part


def doc_starts(lengths, positions):
    doc_ends = jnp.cumsum(lengths)
    return jnp.sum(jnp.where(doc_ends[None, :] <= positions[:, None], lengths[None, :], 0), axis=1)


def local(tokens, doc_lengths, gain_one, w_qkv, w_out, gain_two, w_gate_up, w_down, cotangent):
    token_count = tokens.shape[0]
    device = lax.axis_index("seq")
    chips = lax.axis_size("seq") // 2
    core = device % 2
    chip = device // 2
    place = jnp.where(chip % 2 == 0, chip // 2, chips - (chip + 1) // 2)
    row_length = token_count * lax.axis_size("seq") // doc_lengths.shape[0]
    first = (device * token_count) % row_length
    positions = first + jnp.arange(token_count, dtype=jnp.int32)
    starts = (doc_starts(doc_lengths[0], positions) - first).reshape(token_count, 1)
    f32 = jnp.float32
    bf16 = jnp.bfloat16

    local_width = w_qkv.shape[2]
    qkv_width = 3 * local_width
    rest_width = qkv_width + local_width
    first_own = jnp.concatenate(
        [w_qkv.reshape(-1, qkv_width), w_out.T, w_down.T], axis=1
    )
    gains = jnp.stack([gain_one, gain_two])
    first_own, second_own, gains = lax.optimization_barrier((first_own, w_gate_up, gains))
    first_weights = lax.all_gather(first_own, "seq", axis=0, tiled=True)
    gate_up_full = lax.all_gather(second_own, "seq", axis=0, tiled=True)
    gains = gather_small(gains).astype(f32)
    gain_a = gains[0]
    gain_b = gains[1]
    qkv_full = first_weights[:, :qkv_width]
    out_full = first_weights[:, qkv_width:rest_width]
    down_full = first_weights[:, rest_width:]

    token_rows = tokens.astype(f32)
    normed = rms_scale(token_rows, gain_a).astype(bf16)
    cot_pair = pair_columns(cotangent, chips, core)
    normed_pair = pair_columns(normed, chips, core)
    proj = jnp.dot(normed, qkv_full, preferred_element_type=f32).astype(bf16)
    last = proj[token_count - WINDOW :]
    last = jnp.stack([last[:, local_width : 2 * local_width], last[:, 2 * local_width :]])
    before = shifted(last, "seq", 1)
    attn_mixed = attend(starts, proj, before)
    attn_out = tp_sum(jnp.einsum("tf,df->td", attn_mixed, out_full, preferred_element_type=f32))
    middle = token_rows + attn_out
    normed_two = rms_scale(middle, gain_b).astype(bf16)
    normed_two_pair = pair_columns(normed_two, chips, core)
    mixed_two = partner(attn_mixed[None])
    grad_hidden = jnp.einsum("td,df->tf", cotangent, down_full, preferred_element_type=f32)
    early = (cot_pair, normed_pair, normed_two_pair, mixed_two, grad_hidden, normed_two)
    early, gate_up_full = lax.optimization_barrier((early, gate_up_full))
    cot_pair, normed_pair, normed_two_pair, mixed_two, grad_hidden, normed_two = early

    gate_up = jnp.einsum("td,dcf->ctf", normed_two, gate_up_full, preferred_element_type=f32)
    hidden = gated(gate_up[0], gate_up[1]).astype(bf16)
    unused_value, gate_pull = jax.vjp(gated, gate_up[0], gate_up[1])
    grad_gate_up = jnp.stack(gate_pull(grad_hidden)).astype(bf16)

    def through_gate_up(grad_gate_up):
        return jnp.einsum(
            "ctf,dcf->td", grad_gate_up, gate_up_full, preferred_element_type=f32
        ).astype(bf16)

    swaps = [to_partner(hidden[None]), to_partner(grad_gate_up)]
    sent_two, (hidden_two, grad_gate_up_two) = beside([], swaps, through_gate_up, grad_gate_up)

    def down_product(hidden):
        return pair_terms(cot_pair, row_major(hidden[None]), row_major(hidden_two), chips)

    down_terms, (part_a,) = beside([], [tp_rows(sent_two, 0, 1)], down_product, hidden)
    down = Ring(down_terms, chips, place)

    def gate_up_product(grad_gate_up):
        right = row_major(grad_gate_up), row_major(grad_gate_up_two)
        return pair_terms(normed_two_pair, *right, chips)

    gate_up_terms, (part_b,) = beside(
        [down], [tp_rows(sent_two, 1, 3)], gate_up_product, grad_gate_up
    )
    gate_up_ring = Ring(gate_up_terms, chips, place)
    rings = [down, gate_up_ring]

    def through_down(hidden):
        return jnp.einsum("tf,df->td", hidden, down_full, preferred_element_type=f32).astype(bf16)

    sent_branch, (part_c,) = beside(rings, [tp_rows(sent_two, 3, 4)], through_down, hidden)
    grad_normed_two = tp_join(sent_two, [part_a, part_b, part_c])

    def through_norm_two(middle):
        unused_norm, norm_pull = jax.vjp(rms_scale, middle, gain_b)
        grad_mid_norm, grad_gain_two = norm_pull(grad_normed_two)
        grad_middle = cotangent.astype(f32) + grad_mid_norm
        grad_attn = grad_middle.astype(bf16)
        grad_mixed = jnp.einsum("td,df->tf", grad_attn, out_full, preferred_element_type=f32)
        return grad_middle, grad_gain_two, grad_attn, grad_mixed.astype(bf16)

    made, (branch_a,) = beside(rings, [tp_rows(sent_branch, 0, 2)], through_norm_two, middle)
    grad_middle, grad_gain_two, grad_attn, grad_mixed = made
    grad_gain_two = scatter_small(grad_gain_two)

    def through_attention(grad_mixed, grad_attn):
        grad_attn_pair = pair_columns(grad_attn, chips, core)
        return grad_attn_pair, attend_back(starts, proj, before, grad_mixed)

    made, (branch_b,) = beside(
        rings, [tp_rows(sent_branch, 2, 4)], through_attention, grad_mixed, grad_attn
    )
    grad_attn_pair, (grad_queries, grad_keys, grad_values, rim, tail) = made
    branch = tp_join(sent_branch, [branch_a, branch_b])
    size = 2 * chips
    back_route = [(i + 1, i) for i in range(size - 1)]

    def out_product(attn_mixed):
        return pair_terms(grad_attn_pair, attn_mixed[None], mixed_two, chips)

    out_terms, (arrived,) = beside(rings, [(rim, "seq", back_route)], out_product, attn_mixed)
    rings.append(Ring(out_terms, chips, place))

    def through_qkv(grad_queries):
        edge = (tail + arrived.astype(f32)).astype(bf16)
        inner = token_count - WINDOW
        whole_keys = jnp.concatenate([grad_keys[:inner], edge[0]])
        whole_values = jnp.concatenate([grad_values[:inner], edge[1]])
        grad_proj = jnp.concatenate([grad_queries, whole_keys, whole_values], axis=1)
        sent = jnp.einsum("tf,df->td", grad_proj, qkv_full, preferred_element_type=f32)
        return grad_proj, sent.astype(bf16)

    (grad_proj, sent_one), unused_none = beside(rings, [], through_qkv, grad_queries)

    def finish(middle):
        return (middle + branch).astype(bf16)

    result, (grad_proj_two, part_a) = beside(
        rings, [to_partner(grad_proj[None]), tp_rows(sent_one, 0, 2)], finish, middle
    )

    def qkv_product(grad_proj):
        return pair_terms(normed_pair, grad_proj[None], grad_proj_two, chips)

    qkv_terms, (part_b,) = beside(rings, [tp_rows(sent_one, 2, 4)], qkv_product, grad_proj)
    rings.append(Ring(qkv_terms, chips, place))
    grad_normed = tp_join(sent_one, [part_a, part_b])

    def through_norm(token_rows):
        unused_first, first_pull = jax.vjp(rms_scale, token_rows, gain_a)
        grad_rows_norm, grad_gain_one = first_pull(grad_normed)
        return grad_middle + grad_rows_norm, grad_gain_one

    (grad_tokens, grad_gain_one), unused_none = beside(rings, [], through_norm, token_rows)
    grad_gain_one = scatter_small(grad_gain_one)

    def finish_down(whole):
        return whole[0].T

    def finish_gate_up(whole):
        return whole.transpose(1, 0, 2)

    grad_w_down, unused_none = beside(rings, [], finish_down, down.result())
    grad_w_gate_up, unused_none = beside(rings, [], finish_gate_up, gate_up_ring.result())
    grad_w_out = rings[2].result()[0].T
    grad_w_qkv = rings[3].result().reshape(-1, 3, local_width)
    return (
        result,
        grad_tokens,
        grad_gain_one,
        grad_w_qkv,
        grad_w_out,
        grad_gain_two,
        grad_w_gate_up,
        grad_w_down,
    )


def solution(mesh):
    return jax.shard_map(
        local,
        mesh=mesh,
        in_specs=(
            P("seq", None),
            P(),
            P("seq"),
            P("seq", None, "tp"),
            P("tp", "seq"),
            P("seq"),
            P("seq", None, "tp"),
            P("tp", "seq"),
            P("seq", None),
        ),
        out_specs=(
            P("seq", None),
            P("seq", None),
            P("seq"),
            P("seq", None, "tp"),
            P("tp", "seq"),
            P("seq"),
            P("seq", None, "tp"),
            P("tp", "seq"),
        ),
        check_vma=False,
    )
```
